512 devices in a mesh: blk: 64 (over y, z_hi, x, core), group: 8 (over z_lo).
Axes of the slice: x: 4, y: 4, z: 16 (z_hi: 2, z_lo: 8; z = z_hi * 8 + z_lo), core: 2. Of those that a mesh axis runs over, the one named last changes fastest.
Arguments:
- sketch: bfloat16 [32768, 768], P('blk'), may hold values from -6 to 6
- far_tiles: bfloat16 [64, 8, 3, 6, 128, 512], P('blk', 'group'), may hold values from -0.1875 to 0.1875
- row_blocks: int32 [64, 8, 3, 6], P('blk', 'group'), may hold values from 0 to 7, as said below
- owner_route: int32 [64, 8, 8], P('blk', 'group'), may hold values from 0 to 7, each once within a row
- cluster_basis: bfloat16 [64, 8, 1024, 256], P('blk', 'group'), may hold values from -0.1875 to 0.1875
Outputs:
- coefficients: float32 [64, 8, 256, 768], P('blk', 'group')
The draws below stay inside these ranges and needn't reach their ends.
Inputs may be any that keep to these rules, and one draw needn't show every extreme that they name: `row_blocks`: for one device and one offset, the 6 entries are distinct. `owner_route`: for each device the entries are a permutation of 0 .. 8 - 1.
All inputs are finite; a program needn't handle non-finite values.
Results may differ from the reference program's by a relative error of at most 0.0029.
Values may be sent and summed in bfloat16 or wider, within the bound.
A program may use at most 64 MiB of HBM per device.

```python
import jax
import jax.numpy as jnp
from jax import lax

K = 768
CL = 1024
RANK = 256
PW = 512
REACH = 1
OFFS = 3
TB = 128
TPO = 6
NCAT = 32768
N_BLK = 64
N_GROUP = 8


def draw_row_blocks(key, part):
    scores = jax.random.randint(key, (N_BLK, N_GROUP, OFFS, N_GROUP), 0, 1 << 20) * N_GROUP
    scores = scores + jnp.arange(N_GROUP, dtype=jnp.int32)
    order = jnp.argsort(scores, axis=-1, stable=True)
    return order[..., :TPO].astype(jnp.int32)


def block_scale(stream_key, shape, split, least, high):
    def one(dim, parts):
        steps = jax.random.uniform(jax.random.fold_in(jax.random.fold_in(stream_key, 6), dim), (parts,), jnp.float32, least / len(split), high / len(split))
        return jnp.repeat(jnp.exp(steps), shape[dim] // parts).reshape((-1,) + (1,) * (len(shape) - dim - 1))

    gain = one(*split[0])
    for cut in split[1:]:
        gain = gain * one(*cut)
    return gain


def scatter_about(key, shape, scale, most, split=(), kind=jnp.bfloat16):
    gain = block_scale(key, shape, split, -0.22, 0.18) if split else 1.0
    drawn = jax.random.normal(key, shape, jnp.float32) * scale * gain
    return jnp.minimum(jnp.maximum(drawn, -most), most).astype(kind)


def setup_inputs(seed: int = 0) -> dict:
    streams_of = jax.random.split(jax.random.key(seed), 6)
    return {
        "sketch": scatter_about(streams_of[0], (NCAT, K), 1.0, 6.0, ((0, 64),)),
        "far_tiles": scatter_about(streams_of[1], (N_BLK, N_GROUP, OFFS, TPO, TB, PW), (2 * PW) ** -0.5, 0.1875, ((0, 64), (1, 8))),
        "row_blocks": draw_row_blocks(jax.random.fold_in(streams_of[5], 71), 0),
        "owner_route": jax.vmap(lambda own: jax.random.permutation(own, N_GROUP))(jax.random.split(streams_of[3], N_BLK * N_GROUP)).reshape((N_BLK, N_GROUP, N_GROUP)).astype(jnp.int32),
        "cluster_basis": scatter_about(streams_of[4], (N_BLK, N_GROUP, CL, RANK), CL ** -0.5, 0.1875, ((0, 64), (1, 8))),
    }


def device_rows(tiles_dev, blocks_dev, panels):
    summed = jnp.zeros((N_GROUP, TB, K), jnp.float32)
    for offset in range(OFFS):
        product = jnp.einsum('trk,kc->trc', tiles_dev[offset].astype(jnp.float32), panels[offset].astype(jnp.float32))
        summed = summed.at[blocks_dev[offset]].add(product)
    return summed.astype(jnp.bfloat16)


def place_rows(rows_dev, route_dev):
    return jnp.zeros_like(rows_dev).at[route_dev].set(rows_dev)


def reference(sketch, far_tiles, row_blocks, owner_route, cluster_basis):
    sketch_blocks = sketch.reshape(N_BLK, PW, K)

    def one_blk(blk_index):
        shifts = jnp.arange(OFFS, dtype=jnp.int32) - REACH
        which = ((blk_index + shifts) % N_BLK).astype(jnp.int32)
        panels = jnp.take(sketch_blocks, which, axis=0)
        sampled = jax.vmap(device_rows, in_axes=(0, 0, None))(far_tiles[blk_index], row_blocks[blk_index], panels)
        ordered = jax.vmap(place_rows)(sampled, owner_route[blk_index])
        cluster = jnp.transpose(ordered, (1, 0, 2, 3)).reshape(N_GROUP, CL, K)
        return jnp.einsum('dlr,dlc->drc', cluster_basis[blk_index].astype(jnp.float32), cluster.astype(jnp.float32))

    return lax.map(one_blk, jnp.arange(N_BLK, dtype=jnp.int32))
```

```python
import functools

import jax
import jax.numpy as jnp
from jax import lax
from jax.experimental import pallas as pl
from jax.experimental.pallas import tpu as pltpu
from jax.sharding import PartitionSpec as P

MESH = pl.DeviceIdType.MESH
ROW = 8
WIDTH = 128
BAND = 256


def kernel(
    blks, groups,
    sketch, far_tiles, row_blocks, owner_route, cluster_basis, out,
    window, tiles, lefts, ordered, received, basis, basis_t,
    in_sem, halo_send, halo_recv, relay_send, block_send, block_recv,
):
    b = lax.axis_index("blk")
    g = lax.axis_index("group")
    offsets, slots, tile_rows, panels = far_tiles.shape[2:]
    chunks = window.shape[0]
    half = groups // 2
    low, high = lax.rem(b, ROW) == 0, lax.rem(b, ROW) == ROW - 1
    end = (g == 0) | (g == groups - 1)
    before = (lax.rem(b + blks - 1, blks), jnp.where(low, groups - 1 - g, g))
    after = (lax.rem(b + 1, blks), jnp.where(high, groups - 1 - g, g))
    sends_before = jnp.logical_not(low) | end
    sends_after = jnp.logical_not(high) | end
    inward = (b, jnp.where(g < half, g + 1, g - 1))
    passes_on = (g != half - 1) & (g != half)

    def own_chunk(k):
        return pltpu.make_async_copy(
            sketch.at[:, pl.ds(k * WIDTH, WIDTH)], window.at[k, 1], in_sem.at[k]
        )

    tiles_in = pltpu.make_async_copy(
        far_tiles.at[0, 0], tiles.at[:, pl.ds(0, slots)], in_sem.at[chunks]
    )
    basis_in = pltpu.make_async_copy(cluster_basis.at[0, 0], basis, in_sem.at[chunks + 1])

    def to_before(k):
        return pltpu.make_async_remote_copy(
            src_ref=window.at[k, 1], dst_ref=window.at[k, 2],
            send_sem=halo_send.at[0, k], recv_sem=halo_recv.at[1, k],
            device_id=before, device_id_type=MESH,
        )

    def to_after(k):
        return pltpu.make_async_remote_copy(
            src_ref=window.at[k, 1], dst_ref=window.at[k, 0],
            send_sem=halo_send.at[1, k], recv_sem=halo_recv.at[0, k],
            device_id=after, device_id_type=MESH,
        )

    def relay(k, place):
        return pltpu.make_async_remote_copy(
            src_ref=window.at[k, place], dst_ref=window.at[k, place],
            send_sem=relay_send.at[k], recv_sem=halo_recv.at[place // 2, k],
            device_id=inward, device_id_type=MESH,
        )

    def block(k, owner):
        return pltpu.make_async_remote_copy(
            src_ref=ordered.at[k, owner], dst_ref=received.at[k, g],
            send_sem=block_send.at[k, owner], recv_sem=block_recv.at[k, g],
            device_id=(b, owner), device_id_type=MESH,
        )

    def from_peer(k, peer):
        return pltpu.make_async_remote_copy(
            src_ref=ordered.at[k, peer], dst_ref=received.at[k, peer],
            send_sem=block_send.at[k, peer], recv_sem=block_recv.at[k, peer],
            device_id=(b, peer), device_id_type=MESH,
        )

    barrier = pltpu.get_barrier_semaphore()
    for step in range(1, groups):
        pl.semaphore_signal(
            barrier, inc=1, device_id=(b, lax.rem(g + step, groups)), device_id_type=MESH
        )

    @pl.when(sends_before)
    def _():
        pl.semaphore_signal(barrier, inc=1, device_id=before, device_id_type=MESH)

    @pl.when(sends_after)
    def _():
        pl.semaphore_signal(barrier, inc=1, device_id=after, device_id_type=MESH)

    for k in range(chunks):
        own_chunk(k).start()
    tiles_in.start()
    basis_in.start()
    tiles[:, slots] = jnp.zeros((offsets, tile_rows, panels), tiles.dtype)

    pl.semaphore_wait(
        barrier, groups - 1 + sends_before.astype(jnp.int32) + sends_after.astype(jnp.int32)
    )

    for k in range(chunks):
        own_chunk(k).wait()

        @pl.when(sends_before)
        def _():
            to_before(k).start()

        @pl.when(sends_after)
        def _():
            to_after(k).start()

    tiles_in.wait()
    for offset in range(offsets):
        owners = [owner_route[row_blocks[offset, slot]] for slot in range(slots)]
        for owner in range(groups):
            slot = jnp.int32(slots)
            for candidate in range(slots):
                slot = jnp.where(owners[candidate] == owner, candidate, slot)
            lefts[
                pl.ds(owner * tile_rows, tile_rows), pl.ds(offset * panels, panels)
            ] = tiles[offset, slot]

    per_band = BAND // tile_rows
    bands = groups // per_band

    def sample(k, _):
        pltpu.make_async_remote_copy(
            src_ref=window.at[k, 1], dst_ref=window.at[k, 0],
            send_sem=halo_send.at[1, k], recv_sem=halo_recv.at[0, k],
            device_id=after, device_id_type=MESH,
        ).wait_recv()

        @pl.when(low & passes_on)
        def _():
            relay(k, 0).start()

        pltpu.make_async_remote_copy(
            src_ref=window.at[k, 1], dst_ref=window.at[k, 2],
            send_sem=halo_send.at[0, k], recv_sem=halo_recv.at[1, k],
            device_id=before, device_id_type=MESH,
        ).wait_recv()

        @pl.when(high & passes_on)
        def _():
            relay(k, 2).start()

        panels_in = window[k].reshape(offsets * panels, WIDTH)

        def band(step, _):
            place = lax.rem(step + jnp.where(g < half, bands // 2, 0), bands)
            rows = jnp.dot(
                lefts[pl.ds(pl.multiple_of(place * BAND, BAND), BAND), :],
                panels_in,
                preferred_element_type=jnp.float32,
            ).astype(jnp.bfloat16)
            for part in range(per_band):
                owner = place * per_band + part
                ordered[k, owner] = rows[part * tile_rows : (part + 1) * tile_rows]

                @pl.when(owner != g)
                def _():
                    block(k, owner).start()

            return 0

        lax.fori_loop(0, bands, band, 0)
        received[k, g] = ordered[k, g]
        return 0

    lax.fori_loop(0, chunks, sample, 0)

    basis_in.wait()
    basis_t[...] = basis[...].T

    for k in range(chunks):

        def arrive(step, _):
            from_peer(k, lax.rem(g + step, groups)).wait_recv()
            return 0

        lax.fori_loop(1, groups, arrive, 0)
        out[:, k * WIDTH : (k + 1) * WIDTH] = jnp.dot(
            basis_t[...],
            received[k].reshape(groups * tile_rows, WIDTH),
            preferred_element_type=jnp.float32,
        )

    def drain(k, _):
        def left(step, _):
            block(k, lax.rem(g + step, groups)).wait_send()
            return 0

        lax.fori_loop(1, groups, left, 0)

        @pl.when(sends_before)
        def _():
            to_before(k).wait_send()

        @pl.when(sends_after)
        def _():
            to_after(k).wait_send()

        @pl.when(low & passes_on)
        def _():
            relay(k, 0).wait_send()

        @pl.when(high & passes_on)
        def _():
            relay(k, 2).wait_send()

        return 0

    lax.fori_loop(0, chunks, drain, 0)


def solution(mesh):
    blks, groups = mesh.shape["blk"], mesh.shape["group"]

    def body(sketch, far_tiles, row_blocks, owner_route, cluster_basis):
        offsets, slots, tile_rows, panels = far_tiles.shape[2:]
        columns = sketch.shape[1]
        cluster_rows, rank = cluster_basis.shape[2:]
        chunks = columns // WIDTH
        kept = jnp.bfloat16
        coefficients = pl.pallas_call(
            functools.partial(kernel, blks, groups),
            out_shape=jax.ShapeDtypeStruct((rank, columns), jnp.float32),
            in_specs=[
                pl.BlockSpec(memory_space=pl.ANY),
                pl.BlockSpec(memory_space=pl.ANY),
                pl.BlockSpec(memory_space=pltpu.SMEM),
                pl.BlockSpec(memory_space=pltpu.SMEM),
                pl.BlockSpec(memory_space=pl.ANY),
            ],
            out_specs=pl.BlockSpec(memory_space=pltpu.VMEM),
            scratch_shapes=[
                pltpu.VMEM((chunks, offsets, panels, WIDTH), kept),
                pltpu.VMEM((offsets, slots + 1, tile_rows, panels), kept),
                pltpu.VMEM((groups * tile_rows, offsets * panels), kept),
                pltpu.VMEM((chunks, groups, tile_rows, WIDTH), kept),
                pltpu.VMEM((chunks, groups, tile_rows, WIDTH), kept),
                pltpu.VMEM((cluster_rows, rank), kept),
                pltpu.VMEM((rank, cluster_rows), kept),
                pltpu.SemaphoreType.DMA((chunks + 2,)),
                pltpu.SemaphoreType.DMA((2, chunks)),
                pltpu.SemaphoreType.DMA((2, chunks)),
                pltpu.SemaphoreType.DMA((chunks,)),
                pltpu.SemaphoreType.DMA((chunks, groups)),
                pltpu.SemaphoreType.DMA((chunks, groups)),
            ],
            compiler_params=pltpu.CompilerParams(
                collective_id=0, has_side_effects=True, vmem_limit_bytes=60 * 1024 * 1024
            ),
        )(sketch, far_tiles, row_blocks[0, 0], owner_route[0, 0], cluster_basis)
        return coefficients[None, None]

    placed = (
        P("blk", None),
        P("blk", "group", None, None, None, None),
        P("blk", "group", None, None),
        P("blk", "group", None),
        P("blk", "group", None, None),
    )
    return jax.shard_map(
        body, mesh=mesh, in_specs=placed, out_specs=P("blk", "group", None, None), check_vma=False
    )
```

```python
import functools

import jax
import jax.numpy as jnp
from jax import lax
from jax.experimental import pallas as pl
from jax.experimental.pallas import tpu as pltpu
from jax.sharding import PartitionSpec as P

MESH = pl.DeviceIdType.MESH
ROW = 8
WIDTH = 128
BAND = 256
PARTS = (1, 2, 3)


def kernel(
    blks, groups,
    sketch, far_tiles, row_blocks, owner_route, cluster_basis, out,
    window, tiles, lefts, ordered, received, basis, basis_t,
    in_sem, halo_send, halo_recv, edge_send,
    block_send, block_recv,
):
    b = lax.axis_index("blk")
    g = lax.axis_index("group")
    offsets, slots, tile_rows, panels = far_tiles.shape[2:]
    chunks = window.shape[0]
    half = groups // 2
    core = lax.rem(b, 2)
    low, high = lax.rem(b, ROW) == 0, lax.rem(b, ROW) == ROW - 1
    edge = low | high
    end = (g == 0) | (g == groups - 1)
    source = edge & end
    before, after = lax.rem(b + blks - 1, blks), lax.rem(b + 1, blks)
    def own_chunk(k):
        return pltpu.make_async_copy(
            sketch.at[:, pl.ds(k * WIDTH, WIDTH)], window.at[k, 1], in_sem.at[k]
        )

    tiles_in = pltpu.make_async_copy(
        far_tiles.at[0, 0], tiles.at[:, pl.ds(0, slots)], in_sem.at[chunks]
    )
    basis_in = pltpu.make_async_copy(cluster_basis.at[0, 0], basis, in_sem.at[chunks + 1])

    def to_before(k):
        return pltpu.make_async_remote_copy(
            src_ref=window.at[k, 1], dst_ref=window.at[k, 2],
            send_sem=halo_send.at[0, k], recv_sem=halo_recv.at[1, k],
            device_id=(before, g), device_id_type=MESH,
        )

    def to_after(k):
        return pltpu.make_async_remote_copy(
            src_ref=window.at[k, 1], dst_ref=window.at[k, 0],
            send_sem=halo_send.at[1, k], recv_sem=halo_recv.at[0, k],
            device_id=(after, g), device_id_type=MESH,
        )

    def across(k, group):
        return pltpu.make_async_remote_copy(
            src_ref=window.at[k, 1], dst_ref=window.at[k, 2 * (1 - core)],
            send_sem=edge_send.at[k, group % half], recv_sem=halo_recv.at[1 - core, k],
            device_id=(jnp.where(low, before, after), jnp.where(g == 0, group, group - half)),
            device_id_type=MESH,
        )

    starts = [sum(PARTS[:p]) for p in range(len(PARTS))]

    def block(p, owner):
        span = pl.ds(starts[p], PARTS[p])
        return pltpu.make_async_remote_copy(
            src_ref=ordered.at[span, owner], dst_ref=received.at[span, g],
            send_sem=block_send.at[p, owner], recv_sem=block_recv.at[p, g],
            device_id=(b, owner), device_id_type=MESH,
        )

    def from_peer(p, peer):
        span = pl.ds(starts[p], PARTS[p])
        return pltpu.make_async_remote_copy(
            src_ref=ordered.at[span, peer], dst_ref=received.at[span, peer],
            send_sem=block_send.at[p, peer], recv_sem=block_recv.at[p, peer],
            device_id=(b, peer), device_id_type=MESH,
        )

    barrier = pltpu.get_barrier_semaphore()

    def greet(blk, group):
        pl.semaphore_signal(barrier, inc=1, device_id=(blk, group), device_id_type=MESH)

    for step in range(1, groups):
        greet(b, lax.rem(g + step, groups))

    @pl.when(jnp.logical_not(low))
    def _():
        greet(before, g)

    @pl.when(jnp.logical_not(high))
    def _():
        greet(after, g)

    @pl.when(edge)
    def _():
        greet(jnp.where(low, before, after), jnp.where(g < half, groups - 1, 0))

    for k in range(chunks):
        own_chunk(k).start()
    tiles_in.start()
    basis_in.start()
    tiles[:, slots] = jnp.zeros((offsets, tile_rows, panels), tiles.dtype)

    pl.semaphore_wait(
        barrier, groups - 1 + jnp.where(edge, 1, 2) + jnp.where(source, half, 0)
    )

    for k in range(chunks):
        own_chunk(k).wait()

        @pl.when(source)
        def _():
            for group in range(half, groups):
                across(k, group).start()

        @pl.when(jnp.logical_not(low))
        def _():
            to_before(k).start()

        @pl.when(jnp.logical_not(high))
        def _():
            to_after(k).start()

    tiles_in.wait()
    for offset in range(offsets):
        owners = [owner_route[0, 0, row_blocks[0, offset, 0, slot]] for slot in range(slots)]
        for owner in range(groups):
            slot = jnp.int32(slots)
            for candidate in range(slots):
                slot = jnp.where(owners[candidate] == owner, candidate, slot)
            lefts[
                pl.ds(owner * tile_rows, tile_rows), pl.ds(offset * panels, panels)
            ] = tiles[offset, slot]

    per_band = BAND // tile_rows
    bands = groups // per_band

    def sample(k, sent):
        to_after(k).wait_recv()
        to_before(k).wait_recv()
        panels_in = window[k].reshape(offsets * panels, WIDTH)

        def band(step, _):
            at = lax.rem(step + jnp.where(g < half, bands // 2, 0), bands)
            rows = jnp.dot(
                lefts[pl.ds(pl.multiple_of(at * BAND, BAND), BAND), :],
                panels_in,
                preferred_element_type=jnp.float32,
            ).astype(jnp.bfloat16)
            for part in range(per_band):
                owner = at * per_band + part
                ordered[k, owner] = rows[part * tile_rows : (part + 1) * tile_rows]
                if sent is not None:

                    @pl.when(owner != g)
                    def _():
                        block(sent, owner).start()

            return 0

        lax.fori_loop(0, bands, band, 0)
        received[k, g] = ordered[k, g]

        return 0

    for p, count in enumerate(PARTS):
        if count == 1:
            sample(starts[p], p)
            continue
        lax.fori_loop(starts[p], starts[p] + count, lambda k, _: sample(k, None), 0)

        def send(step, _):
            block(p, lax.rem(g + step, groups)).start()
            return 0

        lax.fori_loop(1, groups, send, 0)

    basis_in.wait()
    basis_t[...] = basis[...].T
    out[...] = jnp.zeros_like(out)

    def gather(step, _):
        near = step < half
        peer = jnp.where(g < half, 0, half) + lax.rem(g + step, half)
        peer = jnp.where(near, peer, lax.rem(peer + half, groups))

        @pl.when(step > 0)
        def _():
            for p in range(len(PARTS)):
                from_peer(p, peer).wait_recv()

        part = basis_t[:, pl.ds(pl.multiple_of(peer * tile_rows, tile_rows), tile_rows)]
        for k in range(chunks):
            out[:, k * WIDTH : (k + 1) * WIDTH] += jnp.dot(
                part, received[k, peer], preferred_element_type=jnp.float32
            )
        return 0

    lax.fori_loop(0, groups, gather, 0)

    def drain_block(step, _):
        for p in range(len(PARTS)):
            block(p, lax.rem(g + step, groups)).wait_send()
        return 0

    lax.fori_loop(1, groups, drain_block, 0)

    def drain(k, _):
        @pl.when(source)
        def _():
            for group in range(half, groups):
                across(k, group).wait_send()

        @pl.when(jnp.logical_not(low))
        def _():
            to_before(k).wait_send()

        @pl.when(jnp.logical_not(high))
        def _():
            to_after(k).wait_send()

        return 0

    lax.fori_loop(0, chunks, drain, 0)


def solution(mesh):
    blks, groups = mesh.shape["blk"], mesh.shape["group"]

    def body(sketch, far_tiles, row_blocks, owner_route, cluster_basis):
        offsets, slots, tile_rows, panels = far_tiles.shape[2:]
        columns = sketch.shape[1]
        cluster_rows, rank = cluster_basis.shape[2:]
        chunks = columns // WIDTH
        kept = jnp.bfloat16
        coefficients = pl.pallas_call(
            functools.partial(kernel, blks, groups),
            out_shape=jax.ShapeDtypeStruct((rank, columns), jnp.float32),
            in_specs=[
                pl.BlockSpec(memory_space=pl.ANY),
                pl.BlockSpec(memory_space=pl.ANY),
                pl.BlockSpec(memory_space=pltpu.SMEM),
                pl.BlockSpec(memory_space=pltpu.SMEM),
                pl.BlockSpec(memory_space=pl.ANY),
            ],
            out_specs=pl.BlockSpec(memory_space=pltpu.VMEM),
            scratch_shapes=[
                pltpu.VMEM((chunks, offsets, panels, WIDTH), kept),
                pltpu.VMEM((offsets, slots + 1, tile_rows, panels), kept),
                pltpu.VMEM((groups * tile_rows, offsets * panels), kept),
                pltpu.VMEM((chunks, groups, tile_rows, WIDTH), kept),
                pltpu.VMEM((chunks, groups, tile_rows, WIDTH), kept),
                pltpu.VMEM((cluster_rows, rank), kept),
                pltpu.VMEM((rank, cluster_rows), kept),
                pltpu.SemaphoreType.DMA((chunks + 2,)),
                pltpu.SemaphoreType.DMA((2, chunks)),
                pltpu.SemaphoreType.DMA((2, chunks)),
                pltpu.SemaphoreType.DMA((chunks, groups // 2)),
                pltpu.SemaphoreType.DMA((len(PARTS), groups)),
                pltpu.SemaphoreType.DMA((len(PARTS), groups)),
            ],
            compiler_params=pltpu.CompilerParams(
                collective_id=0, has_side_effects=True, vmem_limit_bytes=60 * 1024 * 1024
            ),
        )(sketch, far_tiles, jnp.transpose(row_blocks, (0, 2, 1, 3)), owner_route, cluster_basis)
        return coefficients[None, None]

    placed = (
        P("blk", None),
        P("blk", "group", None, None, None, None),
        P("blk", "group", None, None),
        P("blk", "group", None),
        P("blk", "group", None, None),
    )
    return jax.shard_map(
        body, mesh=mesh, in_specs=placed, out_specs=P("blk", "group", None, None), check_vma=False
    )
```

```python
import functools

import jax
import jax.numpy as jnp
from jax import lax
from jax.experimental import pallas as pl
from jax.experimental.pallas import tpu as pltpu
from jax.sharding import PartitionSpec as P

MESH = pl.DeviceIdType.MESH
LANES = 4
ROW = 2 * LANES
WIDTH = 128
BAND = 256
PARTS = (1, 2, 3)


def kernel(
    blks, groups,
    sketch, far_tiles, row_blocks, owner_route, cluster_basis, out,
    window, tiles, lefts, ordered, received, basis, basis_t,
    in_sem, halo_send, halo_recv, piece_send, piece_recv, across_send, across_recv,
    block_send, block_recv,
):
    b = lax.axis_index("blk")
    g = lax.axis_index("group")
    offsets, slots, tile_rows, panels = far_tiles.shape[2:]
    chunks = window.shape[0]
    half = groups // 2
    core = lax.rem(b, 2)
    low, high = lax.rem(b, ROW) == 0, lax.rem(b, ROW) == ROW - 1
    edge = low | high
    end = (g == 0) | (g == groups - 1)
    before, after = lax.rem(b + blks - 1, blks), lax.rem(b + 1, blks)
    piece = panels // LANES
    row = b // ROW * ROW
    lane = lax.rem(b, ROW) // 2
    held = jnp.where(edge, 1, offsets)
    splits, forwards = edge & end, end & jnp.logical_not(edge)
    goal = jnp.where(core == 0, lax.rem(row + blks - 1, blks), lax.rem(row + ROW, blks))
    feeders = jnp.where(low, lax.rem(row + blks - ROW, blks), lax.rem(row + ROW, blks)) + 1 - core

    starts = [sum(PARTS[:p]) for p in range(len(PARTS))]

    def own_chunk(k):
        return pltpu.make_async_copy(
            sketch.at[:, pl.ds(k * WIDTH, WIDTH)], window.at[k, 1], in_sem.at[k]
        )

    tiles_in = pltpu.make_async_copy(
        far_tiles.at[0, 0], tiles.at[:, pl.ds(0, slots)], in_sem.at[chunks]
    )
    basis_in = pltpu.make_async_copy(cluster_basis.at[0, 0], basis, in_sem.at[chunks + 1])

    def to_before(k):
        return pltpu.make_async_remote_copy(
            src_ref=window.at[k, 1], dst_ref=window.at[k, 2],
            send_sem=halo_send.at[0, k], recv_sem=halo_recv.at[1, k],
            device_id=(before, g), device_id_type=MESH,
        )

    def to_after(k):
        return pltpu.make_async_remote_copy(
            src_ref=window.at[k, 1], dst_ref=window.at[k, 0],
            send_sem=halo_send.at[1, k], recv_sem=halo_recv.at[0, k],
            device_id=(after, g), device_id_type=MESH,
        )

    def spread(p, step):
        lane_to = lax.rem(lane + step, LANES)
        rows = pl.ds(pl.multiple_of(lane_to * piece, piece), piece)
        span = pl.ds(starts[p], PARTS[p])
        return pltpu.make_async_remote_copy(
            src_ref=window.at[span, 1, rows], dst_ref=window.at[span, offsets, rows],
            send_sem=piece_send.at[p, step], recv_sem=piece_recv.at[p],
            device_id=(row + 2 * lane_to + core, g), device_id_type=MESH,
        )

    def across(p, hop):
        rows = pl.ds(pl.multiple_of(lane * piece, piece), piece)
        span = pl.ds(starts[p], PARTS[p])
        return pltpu.make_async_remote_copy(
            src_ref=window.at[span, held, rows], dst_ref=window.at[span, 2 * (1 - core), rows],
            send_sem=across_send.at[p, hop], recv_sem=across_recv.at[p],
            device_id=(goal, jnp.where(g == 0, half + hop, half - 1 - hop)), device_id_type=MESH,
        )

    def from_across(p):
        span = pl.ds(starts[p], PARTS[p])
        return pltpu.make_async_remote_copy(
            src_ref=window.at[span, 1], dst_ref=window.at[span, 2 * core],
            send_sem=across_send.at[p, 0], recv_sem=across_recv.at[p],
            device_id=(goal, g), device_id_type=MESH,
        )

    def block(p, owner):
        span = pl.ds(starts[p], PARTS[p])
        return pltpu.make_async_remote_copy(
            src_ref=ordered.at[span, owner], dst_ref=received.at[span, g],
            send_sem=block_send.at[p, owner], recv_sem=block_recv.at[p, g],
            device_id=(b, owner), device_id_type=MESH,
        )

    def from_peer(p, peer):
        span = pl.ds(starts[p], PARTS[p])
        return pltpu.make_async_remote_copy(
            src_ref=ordered.at[span, peer], dst_ref=received.at[span, peer],
            send_sem=block_send.at[p, peer], recv_sem=block_recv.at[p, peer],
            device_id=(b, peer), device_id_type=MESH,
        )

    barrier = pltpu.get_barrier_semaphore()

    def greet(blk, group):
        pl.semaphore_signal(barrier, inc=1, device_id=(blk, group), device_id_type=MESH)

    for step in range(1, groups):
        greet(b, lax.rem(g + step, groups))

    @pl.when(jnp.logical_not(low))
    def _():
        greet(before, g)

    @pl.when(jnp.logical_not(high))
    def _():
        greet(after, g)

    @pl.when(edge)
    def _():
        for q in range(LANES):
            greet(feeders + 2 * q, jnp.where(g < half, groups - 1, 0))

    @pl.when(forwards)
    def _():
        greet(row + core * (ROW - 1), g)

    for k in range(chunks):
        own_chunk(k).start()
    tiles_in.start()
    basis_in.start()
    tiles[:, slots] = jnp.zeros((offsets, tile_rows, panels), tiles.dtype)

    pl.semaphore_wait(
        barrier, groups - 1 + jnp.where(edge, 1, 2) + jnp.where(end, half, 0) + jnp.where(splits, LANES - 1, 0)
    )

    for p, count in enumerate(PARTS):
        for k in range(starts[p], starts[p] + count):
            own_chunk(k).wait()

        @pl.when(splits)
        def _():
            for step in range(1, LANES):
                spread(p, step).start()
            for hop in range(half):
                across(p, hop).start()

        for k in range(starts[p], starts[p] + count):

            @pl.when(jnp.logical_not(low))
            def _():
                to_before(k).start()

            @pl.when(jnp.logical_not(high))
            def _():
                to_after(k).start()

    tiles_in.wait()
    for offset in range(offsets):
        owners = [owner_route[0, 0, row_blocks[0, offset, 0, slot]] for slot in range(slots)]
        for owner in range(groups):
            slot = jnp.int32(slots)
            for candidate in range(slots):
                slot = jnp.where(owners[candidate] == owner, candidate, slot)
            lefts[
                pl.ds(owner * tile_rows, tile_rows), pl.ds(offset * panels, panels)
            ] = tiles[offset, slot]

    per_band = BAND // tile_rows
    bands = groups // per_band

    def sample(k, sent):
        @pl.when(jnp.logical_not(low))
        def _():
            to_after(k).wait_recv()

        @pl.when(jnp.logical_not(high))
        def _():
            to_before(k).wait_recv()

        panels_in = window[k, 0:offsets].reshape(offsets * panels, WIDTH)

        def band(step, _):
            at = lax.rem(step + jnp.where(g < half, bands // 2, 0), bands)
            rows = jnp.dot(
                lefts[pl.ds(pl.multiple_of(at * BAND, BAND), BAND), :],
                panels_in,
                preferred_element_type=jnp.float32,
            ).astype(jnp.bfloat16)
            for part in range(per_band):
                owner = at * per_band + part
                ordered[k, owner] = rows[part * tile_rows : (part + 1) * tile_rows]
                if sent is not None:

                    @pl.when(owner != g)
                    def _():
                        block(sent, owner).start()

            return 0

        lax.fori_loop(0, bands, band, 0)
        received[k, g] = ordered[k, g]

        return 0

    for p, count in enumerate(PARTS):

        @pl.when(forwards)
        def _():
            spread(p, 0).wait_recv()
            for hop in range(half):
                across(p, hop).start()

        @pl.when(edge)
        def _():
            from_across(p).wait_recv()

        if count == 1:
            sample(starts[p], p)
            continue
        lax.fori_loop(starts[p], starts[p] + count, lambda k, _: sample(k, None), 0)

        def send(step, _):
            block(p, lax.rem(g + step, groups)).start()
            return 0

        lax.fori_loop(1, groups, send, 0)

    basis_in.wait()
    basis_t[...] = basis[...].T
    out[...] = jnp.zeros_like(out)

    def gather(step, _):
        near = step < half
        peer = jnp.where(g < half, 0, half) + lax.rem(g + step, half)
        peer = jnp.where(near, peer, lax.rem(peer + half, groups))

        @pl.when(step > 0)
        def _():
            for p in range(len(PARTS)):
                from_peer(p, peer).wait_recv()

        part = basis_t[:, pl.ds(pl.multiple_of(peer * tile_rows, tile_rows), tile_rows)]
        for k in range(chunks):
            out[:, k * WIDTH : (k + 1) * WIDTH] += jnp.dot(
                part, received[k, peer], preferred_element_type=jnp.float32
            )
        return 0

    lax.fori_loop(0, groups, gather, 0)

    def drain_block(step, _):
        for p in range(len(PARTS)):
            block(p, lax.rem(g + step, groups)).wait_send()
        return 0

    lax.fori_loop(1, groups, drain_block, 0)

    for p in range(len(PARTS)):

        @pl.when(splits)
        def _():
            for step in range(1, LANES):
                spread(p, step).wait_send()

        @pl.when(end)
        def _():
            for hop in range(half):
                across(p, hop).wait_send()

    def drain(k, _):
        @pl.when(jnp.logical_not(low))
        def _():
            to_before(k).wait_send()

        @pl.when(jnp.logical_not(high))
        def _():
            to_after(k).wait_send()

        return 0

    lax.fori_loop(0, chunks, drain, 0)


def solution(mesh):
    blks, groups = mesh.shape["blk"], mesh.shape["group"]

    def body(sketch, far_tiles, row_blocks, owner_route, cluster_basis):
        offsets, slots, tile_rows, panels = far_tiles.shape[2:]
        columns = sketch.shape[1]
        cluster_rows, rank = cluster_basis.shape[2:]
        chunks = columns // WIDTH
        kept = jnp.bfloat16
        coefficients = pl.pallas_call(
            functools.partial(kernel, blks, groups),
            out_shape=pltpu.VMEM((rank, columns), jnp.float32),
            in_specs=[
                pl.BlockSpec(memory_space=pl.ANY),
                pl.BlockSpec(memory_space=pl.ANY),
                pl.BlockSpec(memory_space=pltpu.SMEM),
                pl.BlockSpec(memory_space=pltpu.SMEM),
                pl.BlockSpec(memory_space=pl.ANY),
            ],
            out_specs=pl.BlockSpec(memory_space=pltpu.VMEM),
            scratch_shapes=[
                pltpu.VMEM((chunks, offsets + 1, panels, WIDTH), kept),
                pltpu.VMEM((offsets, slots + 1, tile_rows, panels), kept),
                pltpu.VMEM((groups * tile_rows, offsets * panels), kept),
                pltpu.VMEM((chunks, groups, tile_rows, WIDTH), kept),
                pltpu.VMEM((chunks, groups, tile_rows, WIDTH), kept),
                pltpu.VMEM((cluster_rows, rank), kept),
                pltpu.VMEM((rank, cluster_rows), kept),
                pltpu.SemaphoreType.DMA((chunks + 2,)),
                pltpu.SemaphoreType.DMA((2, chunks)),
                pltpu.SemaphoreType.DMA((2, chunks)),
                pltpu.SemaphoreType.DMA((len(PARTS), LANES)),
                pltpu.SemaphoreType.DMA((len(PARTS),)),
                pltpu.SemaphoreType.DMA((len(PARTS), groups // 2)),
                pltpu.SemaphoreType.DMA((len(PARTS),)),
                pltpu.SemaphoreType.DMA((len(PARTS), groups)),
                pltpu.SemaphoreType.DMA((len(PARTS), groups)),
            ],
            compiler_params=pltpu.CompilerParams(
                collective_id=0, has_side_effects=True, vmem_limit_bytes=60 * 1024 * 1024
            ),
        )(sketch, far_tiles, jnp.transpose(row_blocks, (0, 2, 1, 3)), owner_route, cluster_basis)
        return coefficients[None, None]

    placed = (
        P("blk", None),
        P("blk", "group", None, None, None, None),
        P("blk", "group", None, None),
        P("blk", "group", None),
        P("blk", "group", None, None),
    )
    return jax.shard_map(
        body, mesh=mesh, in_specs=placed, out_specs=P("blk", "group", None, None), check_vma=False
    )
```

```python
import functools

import jax
import jax.numpy as jnp
from jax import lax
from jax.experimental import pallas as pl
from jax.experimental.pallas import tpu as pltpu
from jax.sharding import PartitionSpec as P

MESH = pl.DeviceIdType.MESH
LANES = 4
ROW = 2 * LANES
WIDTH = 128
BAND = 256
PARTS = (1, 2, 3)


def kernel(
    blks, groups,
    sketch, far_tiles, row_blocks, owner_route, cluster_basis, out,
    window, tiles, lefts, ordered, received, basis, basis_t,
    in_sem, halo_send, halo_recv, piece_send, piece_recv, across_send, across_recv,
    block_send, block_recv,
):
    b = lax.axis_index("blk")
    g = lax.axis_index("group")
    offsets, slots, tile_rows, panels = far_tiles.shape[2:]
    chunks = window.shape[0]
    half = groups // 2
    core = lax.rem(b, 2)
    low, high = lax.rem(b, ROW) == 0, lax.rem(b, ROW) == ROW - 1
    edge = low | high
    end = (g == 0) | (g == groups - 1)
    before, after = lax.rem(b + blks - 1, blks), lax.rem(b + 1, blks)
    piece = panels // LANES
    row = b // ROW * ROW
    lane = lax.rem(b, ROW) // 2
    held = jnp.where(edge, 1, offsets)
    splits, forwards = edge & end, end & jnp.logical_not(edge)
    goal = jnp.where(core == 0, lax.rem(row + blks - 1, blks), lax.rem(row + ROW, blks))
    feeders = jnp.where(low, lax.rem(row + blks - ROW, blks), lax.rem(row + ROW, blks)) + 1 - core

    starts = [sum(PARTS[:p]) for p in range(len(PARTS))]

    def own_chunk(k):
        return pltpu.make_async_copy(
            sketch.at[:, pl.ds(k * WIDTH, WIDTH)], window.at[k, 1], in_sem.at[k]
        )

    tiles_in = pltpu.make_async_copy(
        far_tiles.at[0, 0], tiles.at[:, pl.ds(0, slots)], in_sem.at[chunks]
    )
    basis_in = pltpu.make_async_copy(cluster_basis.at[0, 0], basis, in_sem.at[chunks + 1])

    def to_before(k):
        return pltpu.make_async_remote_copy(
            src_ref=window.at[k, 1], dst_ref=window.at[k, 2],
            send_sem=halo_send.at[0, k], recv_sem=halo_recv.at[1, k],
            device_id=(before, g), device_id_type=MESH,
        )

    def to_after(k):
        return pltpu.make_async_remote_copy(
            src_ref=window.at[k, 1], dst_ref=window.at[k, 0],
            send_sem=halo_send.at[1, k], recv_sem=halo_recv.at[0, k],
            device_id=(after, g), device_id_type=MESH,
        )

    def spread(p, step):
        lane_to = lax.rem(lane + step, LANES)
        rows = pl.ds(pl.multiple_of(lane_to * piece, piece), piece)
        span = pl.ds(starts[p], PARTS[p])
        return pltpu.make_async_remote_copy(
            src_ref=window.at[span, 1, rows], dst_ref=window.at[span, offsets, rows],
            send_sem=piece_send.at[p, step], recv_sem=piece_recv.at[p],
            device_id=(row + 2 * lane_to + core, g), device_id_type=MESH,
        )

    def across(p, hop):
        rows = pl.ds(pl.multiple_of(lane * piece, piece), piece)
        span = pl.ds(starts[p], PARTS[p])
        return pltpu.make_async_remote_copy(
            src_ref=window.at[span, held, rows], dst_ref=window.at[span, 2 * (1 - core), rows],
            send_sem=across_send.at[p, hop], recv_sem=across_recv.at[p],
            device_id=(goal, jnp.where(g == 0, half + hop, half - 1 - hop)), device_id_type=MESH,
        )

    def from_across(p):
        span = pl.ds(starts[p], PARTS[p])
        return pltpu.make_async_remote_copy(
            src_ref=window.at[span, 1], dst_ref=window.at[span, 2 * core],
            send_sem=across_send.at[p, 0], recv_sem=across_recv.at[p],
            device_id=(goal, g), device_id_type=MESH,
        )

    def block(p, owner):
        span = pl.ds(starts[p], PARTS[p])
        return pltpu.make_async_remote_copy(
            src_ref=ordered.at[span, owner], dst_ref=received.at[span, g],
            send_sem=block_send.at[p, owner], recv_sem=block_recv.at[p, g],
            device_id=(b, owner), device_id_type=MESH,
        )

    def from_peer(p, peer):
        span = pl.ds(starts[p], PARTS[p])
        return pltpu.make_async_remote_copy(
            src_ref=ordered.at[span, peer], dst_ref=received.at[span, peer],
            send_sem=block_send.at[p, peer], recv_sem=block_recv.at[p, peer],
            device_id=(b, peer), device_id_type=MESH,
        )

    for k in range(chunks):
        own_chunk(k).start()
    tiles_in.start()
    barrier = pltpu.get_barrier_semaphore()

    def greet(blk, group):
        pl.semaphore_signal(barrier, inc=1, device_id=(blk, group), device_id_type=MESH)

    @pl.when(jnp.logical_not(low))
    def _():
        greet(before, g)

    @pl.when(jnp.logical_not(high))
    def _():
        greet(after, g)

    @pl.when(edge)
    def _():
        for q in range(LANES):
            greet(feeders + 2 * q, jnp.where(g < half, groups - 1, 0))

    @pl.when(forwards)
    def _():
        greet(row + core * (ROW - 1), g)

    for step in range(1, groups):
        greet(b, lax.rem(g + step, groups))

    basis_in.start()
    tiles[:, slots] = jnp.zeros((offsets, tile_rows, panels), tiles.dtype)

    pl.semaphore_wait(
        barrier, groups - 1 + jnp.where(edge, 1, 2) + jnp.where(end, half, 0) + jnp.where(splits, LANES - 1, 0)
    )

    for p, count in enumerate(PARTS):
        for k in range(starts[p], starts[p] + count):
            own_chunk(k).wait()

        @pl.when(splits)
        def _():
            for step in range(1, LANES):
                spread(p, step).start()
            for hop in range(half):
                across(p, hop).start()

        for k in range(starts[p], starts[p] + count):

            @pl.when(jnp.logical_not(low))
            def _():
                to_before(k).start()

            @pl.when(jnp.logical_not(high))
            def _():
                to_after(k).start()

    tiles_in.wait()
    for offset in range(offsets):
        owners = [owner_route[0, 0, row_blocks[0, offset, 0, slot]] for slot in range(slots)]
        for owner in range(groups):
            slot = jnp.int32(slots)
            for candidate in range(slots):
                slot = jnp.where(owners[candidate] == owner, candidate, slot)
            lefts[
                pl.ds(owner * tile_rows, tile_rows), pl.ds(offset * panels, panels)
            ] = tiles[offset, slot]

    per_band = BAND // tile_rows
    bands = groups // per_band

    def sample(k, sent):
        @pl.when(jnp.logical_not(low))
        def _():
            to_after(k).wait_recv()

        @pl.when(jnp.logical_not(high))
        def _():
            to_before(k).wait_recv()

        panels_in = window[k, 0:offsets].reshape(offsets * panels, WIDTH)

        def band(step, _):
            at = lax.rem(step + jnp.where(g < half, bands // 2, 0), bands)
            rows = jnp.dot(
                lefts[pl.ds(pl.multiple_of(at * BAND, BAND), BAND), :],
                panels_in,
                preferred_element_type=jnp.float32,
            ).astype(jnp.bfloat16)
            for part in range(per_band):
                owner = at * per_band + part
                ordered[k, owner] = rows[part * tile_rows : (part + 1) * tile_rows]
                if sent is not None:

                    @pl.when(owner != g)
                    def _():
                        block(sent, owner).start()

            return 0

        lax.fori_loop(0, bands, band, 0)
        received[k, g] = ordered[k, g]

        return 0

    for p, count in enumerate(PARTS):

        @pl.when(forwards)
        def _():
            spread(p, 0).wait_recv()
            for hop in range(half):
                across(p, hop).start()

        @pl.when(edge)
        def _():
            from_across(p).wait_recv()

        if count == 1:
            sample(starts[p], p)
            continue
        lax.fori_loop(starts[p], starts[p] + count, lambda k, _: sample(k, None), 0)

        def send(step, _):
            block(p, lax.rem(g + step, groups)).start()
            return 0

        lax.fori_loop(1, groups, send, 0)

    basis_in.wait()
    basis_t[...] = basis[...].T
    out[...] = jnp.zeros_like(out)

    for p in range(len(PARTS)):

        @pl.when(splits)
        def _():
            for step in range(1, LANES):
                spread(p, step).wait_send()

        @pl.when(end)
        def _():
            for hop in range(half):
                across(p, hop).wait_send()

    def drain(k, _):
        @pl.when(jnp.logical_not(low))
        def _():
            to_before(k).wait_send()

        @pl.when(jnp.logical_not(high))
        def _():
            to_after(k).wait_send()

        return 0

    lax.fori_loop(0, chunks, drain, 0)

    for p, count in enumerate(PARTS):

        def gather(step, _):
            near = step < half
            peer = jnp.where(g < half, 0, half) + lax.rem(g + step, half)
            peer = jnp.where(near, peer, lax.rem(peer + half, groups))

            @pl.when(step > 0)
            def _():
                from_peer(p, peer).wait_recv()

            part = basis_t[:, pl.ds(pl.multiple_of(peer * tile_rows, tile_rows), tile_rows)]
            for k in range(starts[p], starts[p] + count):
                out[:, k * WIDTH : (k + 1) * WIDTH] += jnp.dot(
                    part, received[k, peer], preferred_element_type=jnp.float32
                )
            return 0

        lax.fori_loop(0, groups, gather, 0)

    def drain_block(step, _):
        for p in range(len(PARTS)):
            block(p, lax.rem(g + step, groups)).wait_send()
        return 0

    lax.fori_loop(1, groups, drain_block, 0)


def solution(mesh):
    blks, groups = mesh.shape["blk"], mesh.shape["group"]

    def body(sketch, far_tiles, row_blocks, owner_route, cluster_basis):
        offsets, slots, tile_rows, panels = far_tiles.shape[2:]
        columns = sketch.shape[1]
        cluster_rows, rank = cluster_basis.shape[2:]
        chunks = columns // WIDTH
        kept = jnp.bfloat16
        coefficients = pl.pallas_call(
            functools.partial(kernel, blks, groups),
            out_shape=pltpu.VMEM((rank, columns), jnp.float32),
            in_specs=[
                pl.BlockSpec(memory_space=pl.ANY),
                pl.BlockSpec(memory_space=pl.ANY),
                pl.BlockSpec(memory_space=pltpu.SMEM),
                pl.BlockSpec(memory_space=pltpu.SMEM),
                pl.BlockSpec(memory_space=pl.ANY),
            ],
            out_specs=pl.BlockSpec(memory_space=pltpu.VMEM),
            scratch_shapes=[
                pltpu.VMEM((chunks, offsets + 1, panels, WIDTH), kept),
                pltpu.VMEM((offsets, slots + 1, tile_rows, panels), kept),
                pltpu.VMEM((groups * tile_rows, offsets * panels), kept),
                pltpu.VMEM((chunks, groups, tile_rows, WIDTH), kept),
                pltpu.VMEM((chunks, groups, tile_rows, WIDTH), kept),
                pltpu.VMEM((cluster_rows, rank), kept),
                pltpu.VMEM((rank, cluster_rows), kept),
                pltpu.SemaphoreType.DMA((chunks + 2,)),
                pltpu.SemaphoreType.DMA((2, chunks)),
                pltpu.SemaphoreType.DMA((2, chunks)),
                pltpu.SemaphoreType.DMA((len(PARTS), LANES)),
                pltpu.SemaphoreType.DMA((len(PARTS),)),
                pltpu.SemaphoreType.DMA((len(PARTS), groups // 2)),
                pltpu.SemaphoreType.DMA((len(PARTS),)),
                pltpu.SemaphoreType.DMA((len(PARTS), groups)),
                pltpu.SemaphoreType.DMA((len(PARTS), groups)),
            ],
            compiler_params=pltpu.CompilerParams(
                collective_id=0, has_side_effects=True, vmem_limit_bytes=60 * 1024 * 1024
            ),
        )(sketch, far_tiles, jnp.transpose(row_blocks, (0, 2, 1, 3)), owner_route, cluster_basis)
        return coefficients[None, None]

    placed = (
        P("blk", None),
        P("blk", "group", None, None, None, None),
        P("blk", "group", None, None),
        P("blk", "group", None),
        P("blk", "group", None, None),
    )
    return jax.shard_map(
        body, mesh=mesh, in_specs=placed, out_specs=P("blk", "group", None, None), check_vma=False
    )
```

```python
import functools

import jax
import jax.numpy as jnp
from jax import lax
from jax.experimental import pallas as pl
from jax.experimental.pallas import tpu as pltpu
from jax.sharding import PartitionSpec as P

MESH = pl.DeviceIdType.MESH
LANES = 4
ROW = 2 * LANES
WIDTH = 128
BAND = 256
PARTS = (1, 2, 3)


def kernel(
    blks, groups,
    sketch, far_tiles, row_blocks, owner_route, cluster_basis, out,
    window, tiles, lefts, ordered, received, basis, basis_t,
    in_sem, halo_send, halo_recv, piece_send, piece_recv, across_send, across_recv,
    block_send, block_recv, present,
):
    b = lax.axis_index("blk")
    g = lax.axis_index("group")
    offsets, slots, tile_rows, panels = far_tiles.shape[2:]
    chunks = window.shape[0]
    half = groups // 2
    core = lax.rem(b, 2)
    low, high = lax.rem(b, ROW) == 0, lax.rem(b, ROW) == ROW - 1
    edge = low | high
    end = (g == 0) | (g == groups - 1)
    before, after = lax.rem(b + blks - 1, blks), lax.rem(b + 1, blks)
    piece = panels // LANES
    row = b // ROW * ROW
    lane = lax.rem(b, ROW) // 2
    held = jnp.where(edge, 1, offsets)
    splits, forwards = edge & end, end & jnp.logical_not(edge)
    goal = jnp.where(core == 0, lax.rem(row + blks - 1, blks), lax.rem(row + ROW, blks))
    feeders = jnp.where(low, lax.rem(row + blks - ROW, blks), lax.rem(row + ROW, blks)) + 1 - core

    flip = lax.rem(row // ROW, 2) == 1
    rank = jnp.where(flip, jnp.where(g < half, g + half, groups - 1 - g), g)

    def at_rank(r):
        return jnp.where(flip, jnp.where(r < half, groups - 1 - r, r - half), r)

    together = (lane == 0) | (lane == LANES - 1)

    starts = [sum(PARTS[:p]) for p in range(len(PARTS))]

    def own_chunk(k):
        return pltpu.make_async_copy(
            sketch.at[:, pl.ds(k * WIDTH, WIDTH)], window.at[k, 1], in_sem.at[k]
        )

    tiles_in = pltpu.make_async_copy(
        far_tiles.at[0, 0], tiles.at[:, pl.ds(0, slots)], in_sem.at[chunks]
    )
    basis_in = pltpu.make_async_copy(cluster_basis.at[0, 0], basis, in_sem.at[chunks + 1])

    def to_before(k):
        return pltpu.make_async_remote_copy(
            src_ref=window.at[k, 1], dst_ref=window.at[k, 2],
            send_sem=halo_send.at[0, k], recv_sem=halo_recv.at[1, k],
            device_id=(before, g), device_id_type=MESH,
        )

    def to_after(k):
        return pltpu.make_async_remote_copy(
            src_ref=window.at[k, 1], dst_ref=window.at[k, 0],
            send_sem=halo_send.at[1, k], recv_sem=halo_recv.at[0, k],
            device_id=(after, g), device_id_type=MESH,
        )

    def spread(p, step):
        lane_to = lax.rem(lane + step, LANES)
        rows = pl.ds(pl.multiple_of(lane_to * piece, piece), piece)
        span = pl.ds(starts[p], PARTS[p])
        return pltpu.make_async_remote_copy(
            src_ref=window.at[span, 1, rows], dst_ref=window.at[span, offsets, rows],
            send_sem=piece_send.at[p, step], recv_sem=piece_recv.at[p],
            device_id=(row + 2 * lane_to + core, g), device_id_type=MESH,
        )

    def across(p, hop):
        rows = pl.ds(pl.multiple_of(lane * piece, piece), piece)
        span = pl.ds(starts[p], PARTS[p])
        return pltpu.make_async_remote_copy(
            src_ref=window.at[span, held, rows], dst_ref=window.at[span, 2 * (1 - core), rows],
            send_sem=across_send.at[p, hop], recv_sem=across_recv.at[p],
            device_id=(goal, jnp.where(g == 0, groups - 1 - hop, hop)), device_id_type=MESH,
        )

    def from_across(p):
        span = pl.ds(starts[p], PARTS[p])
        return pltpu.make_async_remote_copy(
            src_ref=window.at[span, 1], dst_ref=window.at[span, 2 * core],
            send_sem=across_send.at[p, 0], recv_sem=across_recv.at[p],
            device_id=(goal, g), device_id_type=MESH,
        )

    def block(p, owner):
        span = pl.ds(starts[p], PARTS[p])
        return pltpu.make_async_remote_copy(
            src_ref=ordered.at[span, owner], dst_ref=received.at[span, g],
            send_sem=block_send.at[p, owner], recv_sem=block_recv.at[p, g],
            device_id=(b, owner), device_id_type=MESH,
        )

    def from_peer(p, peer):
        span = pl.ds(starts[p], PARTS[p])
        return pltpu.make_async_remote_copy(
            src_ref=ordered.at[span, peer], dst_ref=received.at[span, peer],
            send_sem=block_send.at[p, peer], recv_sem=block_recv.at[p, peer],
            device_id=(b, peer), device_id_type=MESH,
        )

    for k in range(chunks):
        own_chunk(k).start()
    tiles_in.start()
    barrier = pltpu.get_barrier_semaphore()

    def greet(blk, group):
        pl.semaphore_signal(barrier, inc=1, device_id=(blk, group), device_id_type=MESH)

    @pl.when(jnp.logical_not(low))
    def _():
        greet(before, g)

    @pl.when(jnp.logical_not(high))
    def _():
        greet(after, g)

    @pl.when(edge)
    def _():
        for q in range(LANES):
            greet(feeders + 2 * q, jnp.where(g < half, groups - 1, 0))

    @pl.when(forwards)
    def _():
        greet(row + core * (ROW - 1), g)

    for r in range(groups):

        @pl.when((r > rank) | (together & (r < rank)))
        def _():
            greet(b, at_rank(r))

    basis_in.start()
    tiles[:, slots] = jnp.zeros((offsets, tile_rows, panels), tiles.dtype)

    pl.semaphore_wait(
        barrier, jnp.where(together, groups - 1, rank) + jnp.where(edge, 1, 2) + jnp.where(end, half, 0) + jnp.where(splits, LANES - 1, 0)
    )

    for r in range(groups - 1):

        @pl.when((r < rank) & jnp.logical_not(together))
        def _():
            pl.semaphore_signal(
                present.at[g], inc=1, device_id=(b, at_rank(r)), device_id_type=MESH
            )

    for p, count in enumerate(PARTS):
        for k in range(starts[p], starts[p] + count):
            own_chunk(k).wait()

        @pl.when(splits)
        def _():
            for step in range(1, LANES):
                spread(p, step).start()
            for hop in range(half):
                across(p, hop).start()

        for k in range(starts[p], starts[p] + count):

            @pl.when(jnp.logical_not(low))
            def _():
                to_before(k).start()

            @pl.when(jnp.logical_not(high))
            def _():
                to_after(k).start()

    tiles_in.wait()
    for offset in range(offsets):
        owners = [owner_route[0, 0, row_blocks[0, offset, 0, slot]] for slot in range(slots)]
        for owner in range(groups):
            slot = jnp.int32(slots)
            for candidate in range(slots):
                slot = jnp.where(owners[candidate] == owner, candidate, slot)
            lefts[
                pl.ds(owner * tile_rows, tile_rows), pl.ds(offset * panels, panels)
            ] = tiles[offset, slot]

    per_band = BAND // tile_rows
    bands = groups // per_band

    def sample(k, sent):
        @pl.when(jnp.logical_not(low))
        def _():
            to_after(k).wait_recv()

        @pl.when(jnp.logical_not(high))
        def _():
            to_before(k).wait_recv()

        panels_in = window[k, 0:offsets].reshape(offsets * panels, WIDTH)

        if sent is not None:

            def one(r, _):
                owner = jnp.where(
                    together, lax.rem(r + jnp.where(g < half, half, 0), groups), at_rank(r)
                )
                ordered[k, owner] = jnp.dot(
                    lefts[pl.ds(pl.multiple_of(owner * tile_rows, tile_rows), tile_rows), :],
                    panels_in,
                    preferred_element_type=jnp.float32,
                ).astype(jnp.bfloat16)

                @pl.when((r > rank) & jnp.logical_not(together))
                def _():
                    pl.semaphore_wait(present.at[owner], 1)

                @pl.when(owner != g)
                def _():
                    block(sent, owner).start()

                return 0

            lax.fori_loop(0, groups, one, 0)
            received[k, g] = ordered[k, g]
            return 0

        def band(step, _):
            at = lax.rem(step + jnp.where(g < half, bands // 2, 0), bands)
            rows = jnp.dot(
                lefts[pl.ds(pl.multiple_of(at * BAND, BAND), BAND), :],
                panels_in,
                preferred_element_type=jnp.float32,
            ).astype(jnp.bfloat16)
            for part in range(per_band):
                owner = at * per_band + part
                ordered[k, owner] = rows[part * tile_rows : (part + 1) * tile_rows]
            return 0

        lax.fori_loop(0, bands, band, 0)
        received[k, g] = ordered[k, g]

        return 0

    for p, count in enumerate(PARTS):

        @pl.when(forwards)
        def _():
            spread(p, 0).wait_recv()
            for hop in range(half):
                across(p, hop).start()

        @pl.when(edge)
        def _():
            from_across(p).wait_recv()

        if count == 1:
            sample(starts[p], p)
            continue
        lax.fori_loop(starts[p], starts[p] + count, lambda k, _: sample(k, None), 0)

        def send(step, _):
            block(p, lax.rem(g + step, groups)).start()
            return 0

        lax.fori_loop(1, groups, send, 0)

    basis_in.wait()
    basis_t[...] = basis[...].T
    out[...] = jnp.zeros_like(out)

    for p in range(len(PARTS)):

        @pl.when(splits)
        def _():
            for step in range(1, LANES):
                spread(p, step).wait_send()

        @pl.when(end)
        def _():
            for hop in range(half):
                across(p, hop).wait_send()

    def drain(k, _):
        @pl.when(jnp.logical_not(low))
        def _():
            to_before(k).wait_send()

        @pl.when(jnp.logical_not(high))
        def _():
            to_after(k).wait_send()

        return 0

    lax.fori_loop(0, chunks, drain, 0)

    for p, count in enumerate(PARTS):

        def gather(step, _):
            near = step < half
            peer = jnp.where(g < half, 0, half) + lax.rem(g + step, half)
            peer = jnp.where(near, peer, lax.rem(peer + half, groups))

            @pl.when(step > 0)
            def _():
                from_peer(p, peer).wait_recv()

            part = basis_t[:, pl.ds(pl.multiple_of(peer * tile_rows, tile_rows), tile_rows)]
            for k in range(starts[p], starts[p] + count):
                out[:, k * WIDTH : (k + 1) * WIDTH] += jnp.dot(
                    part, received[k, peer], preferred_element_type=jnp.float32
                )
            return 0

        lax.fori_loop(0, groups, gather, 0)

    def drain_block(step, _):
        for p in range(len(PARTS)):
            block(p, lax.rem(g + step, groups)).wait_send()
        return 0

    lax.fori_loop(1, groups, drain_block, 0)


def solution(mesh):
    blks, groups = mesh.shape["blk"], mesh.shape["group"]

    def body(sketch, far_tiles, row_blocks, owner_route, cluster_basis):
        offsets, slots, tile_rows, panels = far_tiles.shape[2:]
        columns = sketch.shape[1]
        cluster_rows, rank = cluster_basis.shape[2:]
        chunks = columns // WIDTH
        kept = jnp.bfloat16
        coefficients = pl.pallas_call(
            functools.partial(kernel, blks, groups),
            out_shape=pltpu.VMEM((rank, columns), jnp.float32),
            in_specs=[
                pl.BlockSpec(memory_space=pl.ANY),
                pl.BlockSpec(memory_space=pl.ANY),
                pl.BlockSpec(memory_space=pltpu.SMEM),
                pl.BlockSpec(memory_space=pltpu.SMEM),
                pl.BlockSpec(memory_space=pl.ANY),
            ],
            out_specs=pl.BlockSpec(memory_space=pltpu.VMEM),
            scratch_shapes=[
                pltpu.VMEM((chunks, offsets + 1, panels, WIDTH), kept),
                pltpu.VMEM((offsets, slots + 1, tile_rows, panels), kept),
                pltpu.VMEM((groups * tile_rows, offsets * panels), kept),
                pltpu.VMEM((chunks, groups, tile_rows, WIDTH), kept),
                pltpu.VMEM((chunks, groups, tile_rows, WIDTH), kept),
                pltpu.VMEM((cluster_rows, rank), kept),
                pltpu.VMEM((rank, cluster_rows), kept),
                pltpu.SemaphoreType.DMA((chunks + 2,)),
                pltpu.SemaphoreType.DMA((2, chunks)),
                pltpu.SemaphoreType.DMA((2, chunks)),
                pltpu.SemaphoreType.DMA((len(PARTS), LANES)),
                pltpu.SemaphoreType.DMA((len(PARTS),)),
                pltpu.SemaphoreType.DMA((len(PARTS), groups // 2)),
                pltpu.SemaphoreType.DMA((len(PARTS),)),
                pltpu.SemaphoreType.DMA((len(PARTS), groups)),
                pltpu.SemaphoreType.DMA((len(PARTS), groups)),
                pltpu.SemaphoreType.REGULAR((groups,)),
            ],
            compiler_params=pltpu.CompilerParams(
                collective_id=0, has_side_effects=True, vmem_limit_bytes=60 * 1024 * 1024
            ),
        )(sketch, far_tiles, jnp.transpose(row_blocks, (0, 2, 1, 3)), owner_route, cluster_basis)
        return coefficients[None, None]

    placed = (
        P("blk", None),
        P("blk", "group", None, None, None, None),
        P("blk", "group", None, None),
        P("blk", "group", None),
        P("blk", "group", None, None),
    )
    return jax.shard_map(
        body, mesh=mesh, in_specs=placed, out_specs=P("blk", "group", None, None), check_vma=False
    )
```

```python
import functools

import jax
import jax.numpy as jnp
from jax import lax
from jax.experimental import pallas as pl
from jax.experimental.pallas import tpu as pltpu
from jax.sharding import PartitionSpec as P

MESH = pl.DeviceIdType.MESH
LANES = 4
ROW = 2 * LANES
WIDTH = 128
BAND = 256
PARTS = (1, 2, 3)


def kernel(
    blks, groups,
    sketch, far_tiles, row_blocks, owner_route, cluster_basis, out,
    window, tiles, lefts, ordered, received, basis, basis_t,
    in_sem, halo_send, halo_recv, piece_send, piece_recv, across_send, across_recv,
    block_send, block_recv, present,
):
    b = lax.axis_index("blk")
    g = lax.axis_index("group")
    offsets, slots, tile_rows, panels = far_tiles.shape[2:]
    chunks = window.shape[0]
    half = groups // 2
    core = lax.rem(b, 2)
    low, high = lax.rem(b, ROW) == 0, lax.rem(b, ROW) == ROW - 1
    edge = low | high
    end = (g == 0) | (g == groups - 1)
    before, after = lax.rem(b + blks - 1, blks), lax.rem(b + 1, blks)
    piece = panels // LANES
    row = b // ROW * ROW
    lane = lax.rem(b, ROW) // 2
    held = jnp.where(edge, 1, offsets)
    splits, forwards = edge & end, end & jnp.logical_not(edge)
    goal = jnp.where(core == 0, lax.rem(row + blks - 1, blks), lax.rem(row + ROW, blks))
    feeders = jnp.where(low, lax.rem(row + blks - ROW, blks), lax.rem(row + ROW, blks)) + 1 - core

    flip = lax.rem(row // ROW, 2) == 1
    rank = jnp.where(flip, jnp.where(g < half, g + half, groups - 1 - g), g)

    def at_rank(r):
        return jnp.where(flip, jnp.where(r < half, groups - 1 - r, r - half), r)

    together = (lane == 0) | (lane == LANES - 1)

    starts = [sum(PARTS[:p]) for p in range(len(PARTS))]

    def own_chunk(k):
        return pltpu.make_async_copy(
            sketch.at[:, pl.ds(k * WIDTH, WIDTH)], window.at[k, 1], in_sem.at[k]
        )

    tiles_in = pltpu.make_async_copy(
        far_tiles.at[0, 0], tiles.at[:, pl.ds(0, slots)], in_sem.at[chunks]
    )
    basis_in = pltpu.make_async_copy(cluster_basis.at[0, 0], basis, in_sem.at[chunks + 1])

    def to_before(k):
        return pltpu.make_async_remote_copy(
            src_ref=window.at[k, 1], dst_ref=window.at[k, 2],
            send_sem=halo_send.at[0, k], recv_sem=halo_recv.at[1, k],
            device_id=(before, g), device_id_type=MESH,
        )

    def to_after(k):
        return pltpu.make_async_remote_copy(
            src_ref=window.at[k, 1], dst_ref=window.at[k, 0],
            send_sem=halo_send.at[1, k], recv_sem=halo_recv.at[0, k],
            device_id=(after, g), device_id_type=MESH,
        )

    def spread(p, step):
        lane_to = lax.rem(lane + step, LANES)
        rows = pl.ds(pl.multiple_of(lane_to * piece, piece), piece)
        span = pl.ds(starts[p], PARTS[p])
        return pltpu.make_async_remote_copy(
            src_ref=window.at[span, 1, rows], dst_ref=window.at[span, offsets, rows],
            send_sem=piece_send.at[p, step], recv_sem=piece_recv.at[p],
            device_id=(row + 2 * lane_to + core, g), device_id_type=MESH,
        )

    def across(p, hop):
        rows = pl.ds(pl.multiple_of(lane * piece, piece), piece)
        span = pl.ds(starts[p], PARTS[p])
        return pltpu.make_async_remote_copy(
            src_ref=window.at[span, held, rows], dst_ref=window.at[span, 2 * (1 - core), rows],
            send_sem=across_send.at[p, hop], recv_sem=across_recv.at[p],
            device_id=(goal, jnp.where(g == 0, groups - 1 - hop, hop)), device_id_type=MESH,
        )

    def from_across(p):
        span = pl.ds(starts[p], PARTS[p])
        return pltpu.make_async_remote_copy(
            src_ref=window.at[span, 1], dst_ref=window.at[span, 2 * core],
            send_sem=across_send.at[p, 0], recv_sem=across_recv.at[p],
            device_id=(goal, g), device_id_type=MESH,
        )

    def block(p, owner):
        span = pl.ds(starts[p], PARTS[p])
        return pltpu.make_async_remote_copy(
            src_ref=ordered.at[span, owner], dst_ref=received.at[span, g],
            send_sem=block_send.at[p, owner], recv_sem=block_recv.at[p, g],
            device_id=(b, owner), device_id_type=MESH,
        )

    def from_peer(p, peer):
        span = pl.ds(starts[p], PARTS[p])
        return pltpu.make_async_remote_copy(
            src_ref=ordered.at[span, peer], dst_ref=received.at[span, peer],
            send_sem=block_send.at[p, peer], recv_sem=block_recv.at[p, peer],
            device_id=(b, peer), device_id_type=MESH,
        )

    for k in range(chunks):
        own_chunk(k).start()
    tiles_in.start()
    barrier = pltpu.get_barrier_semaphore()

    def greet(blk, group):
        pl.semaphore_signal(barrier, inc=1, device_id=(blk, group), device_id_type=MESH)

    @pl.when(jnp.logical_not(low))
    def _():
        greet(before, g)

    @pl.when(jnp.logical_not(high))
    def _():
        greet(after, g)

    @pl.when(edge)
    def _():
        for q in range(LANES):
            greet(feeders + 2 * q, jnp.where(g < half, groups - 1, 0))

    @pl.when(forwards)
    def _():
        greet(row + core * (ROW - 1), g)

    for r in range(groups):

        @pl.when((r > rank) | (together & (r < rank)))
        def _():
            greet(b, at_rank(r))

    basis_in.start()
    tiles[:, slots] = jnp.zeros((offsets, tile_rows, panels), tiles.dtype)

    pl.semaphore_wait(
        barrier, jnp.where(together, groups - 1, rank) + jnp.where(edge, 1, 2) + jnp.where(end, half, 0) + jnp.where(splits, LANES - 1, 0)
    )

    for r in range(groups - 1):

        @pl.when((r < rank) & jnp.logical_not(together))
        def _():
            pl.semaphore_signal(
                present.at[g], inc=1, device_id=(b, at_rank(r)), device_id_type=MESH
            )

    for p, count in enumerate(PARTS):
        for k in range(starts[p], starts[p] + count):
            own_chunk(k).wait()

        @pl.when(splits)
        def _():
            for step in range(1, LANES):
                spread(p, step).start()
            for hop in range(half):
                across(p, hop).start()

        for k in range(starts[p], starts[p] + count):

            @pl.when(jnp.logical_not(low))
            def _():
                to_before(k).start()

            @pl.when(jnp.logical_not(high))
            def _():
                to_after(k).start()

    tiles_in.wait()
    for offset in range(offsets):
        owners = [owner_route[0, 0, row_blocks[0, offset, 0, slot]] for slot in range(slots)]
        for owner in range(groups):
            slot = jnp.int32(slots)
            for candidate in range(slots):
                slot = jnp.where(owners[candidate] == owner, candidate, slot)
            lefts[
                pl.ds(owner * tile_rows, tile_rows), pl.ds(offset * panels, panels)
            ] = tiles[offset, slot]

    per_band = BAND // tile_rows
    bands = groups // per_band

    def sample(k, sent):
        @pl.when(jnp.logical_not(low))
        def _():
            to_after(k).wait_recv()

        @pl.when(jnp.logical_not(high))
        def _():
            to_before(k).wait_recv()

        panels_in = window[k, 0:offsets].reshape(offsets * panels, WIDTH)

        if sent is not None:

            def one(r, _):
                owner = jnp.where(
                    together, lax.rem(r + jnp.where(g < half, half, 0), groups), at_rank(r)
                )
                ordered[k, owner] = jnp.dot(
                    lefts[pl.ds(pl.multiple_of(owner * tile_rows, tile_rows), tile_rows), :],
                    panels_in,
                    preferred_element_type=jnp.float32,
                ).astype(jnp.bfloat16)

                @pl.when((r > rank) & jnp.logical_not(together))
                def _():
                    pl.semaphore_wait(present.at[owner], 1)

                @pl.when(owner != g)
                def _():
                    block(sent, owner).start()

                return 0

            lax.fori_loop(0, groups, one, 0)
            received[k, g] = ordered[k, g]
            return 0

        def band(step, _):
            at = lax.rem(step + jnp.where(g < half, bands // 2, 0), bands)
            rows = jnp.dot(
                lefts[pl.ds(pl.multiple_of(at * BAND, BAND), BAND), :],
                panels_in,
                preferred_element_type=jnp.float32,
            ).astype(jnp.bfloat16)
            for part in range(per_band):
                owner = at * per_band + part
                ordered[k, owner] = rows[part * tile_rows : (part + 1) * tile_rows]
            return 0

        lax.fori_loop(0, bands, band, 0)
        received[k, g] = ordered[k, g]

        return 0

    for p in range(len(PARTS)):

        @pl.when(forwards)
        def _():
            spread(p, 0).wait_recv()
            for hop in range(half):
                across(p, hop).start()

    for p, count in enumerate(PARTS):

        @pl.when(edge)
        def _():
            from_across(p).wait_recv()

        if count == 1:
            sample(starts[p], p)
            continue
        lax.fori_loop(starts[p], starts[p] + count, lambda k, _: sample(k, None), 0)

        def send(step, _):
            block(p, lax.rem(g + step, groups)).start()
            return 0

        lax.fori_loop(1, groups, send, 0)

    basis_in.wait()
    basis_t[...] = basis[...].T
    out[...] = jnp.zeros_like(out)

    for p in range(len(PARTS)):

        @pl.when(splits)
        def _():
            for step in range(1, LANES):
                spread(p, step).wait_send()

        @pl.when(end)
        def _():
            for hop in range(half):
                across(p, hop).wait_send()

    def drain(k, _):
        @pl.when(jnp.logical_not(low))
        def _():
            to_before(k).wait_send()

        @pl.when(jnp.logical_not(high))
        def _():
            to_after(k).wait_send()

        return 0

    lax.fori_loop(0, chunks, drain, 0)

    for p, count in enumerate(PARTS):

        def gather(step, _):
            near = step < half
            peer = jnp.where(g < half, 0, half) + lax.rem(g + step, half)
            peer = jnp.where(near, peer, lax.rem(peer + half, groups))

            @pl.when(step > 0)
            def _():
                from_peer(p, peer).wait_recv()

            part = basis_t[:, pl.ds(pl.multiple_of(peer * tile_rows, tile_rows), tile_rows)]
            for k in range(starts[p], starts[p] + count):
                out[:, k * WIDTH : (k + 1) * WIDTH] += jnp.dot(
                    part, received[k, peer], preferred_element_type=jnp.float32
                )
            return 0

        lax.fori_loop(0, groups, gather, 0)

    def drain_block(step, _):
        for p in range(len(PARTS)):
            block(p, lax.rem(g + step, groups)).wait_send()
        return 0

    lax.fori_loop(1, groups, drain_block, 0)


def solution(mesh):
    blks, groups = mesh.shape["blk"], mesh.shape["group"]

    def body(sketch, far_tiles, row_blocks, owner_route, cluster_basis):
        offsets, slots, tile_rows, panels = far_tiles.shape[2:]
        columns = sketch.shape[1]
        cluster_rows, rank = cluster_basis.shape[2:]
        chunks = columns // WIDTH
        kept = jnp.bfloat16
        coefficients = pl.pallas_call(
            functools.partial(kernel, blks, groups),
            out_shape=pltpu.VMEM((rank, columns), jnp.float32),
            in_specs=[
                pl.BlockSpec(memory_space=pl.ANY),
                pl.BlockSpec(memory_space=pl.ANY),
                pl.BlockSpec(memory_space=pltpu.SMEM),
                pl.BlockSpec(memory_space=pltpu.SMEM),
                pl.BlockSpec(memory_space=pl.ANY),
            ],
            out_specs=pl.BlockSpec(memory_space=pltpu.VMEM),
            scratch_shapes=[
                pltpu.VMEM((chunks, offsets + 1, panels, WIDTH), kept),
                pltpu.VMEM((offsets, slots + 1, tile_rows, panels), kept),
                pltpu.VMEM((groups * tile_rows, offsets * panels), kept),
                pltpu.VMEM((chunks, groups, tile_rows, WIDTH), kept),
                pltpu.VMEM((chunks, groups, tile_rows, WIDTH), kept),
                pltpu.VMEM((cluster_rows, rank), kept),
                pltpu.VMEM((rank, cluster_rows), kept),
                pltpu.SemaphoreType.DMA((chunks + 2,)),
                pltpu.SemaphoreType.DMA((2, chunks)),
                pltpu.SemaphoreType.DMA((2, chunks)),
                pltpu.SemaphoreType.DMA((len(PARTS), LANES)),
                pltpu.SemaphoreType.DMA((len(PARTS),)),
                pltpu.SemaphoreType.DMA((len(PARTS), groups // 2)),
                pltpu.SemaphoreType.DMA((len(PARTS),)),
                pltpu.SemaphoreType.DMA((len(PARTS), groups)),
                pltpu.SemaphoreType.DMA((len(PARTS), groups)),
                pltpu.SemaphoreType.REGULAR((groups,)),
            ],
            compiler_params=pltpu.CompilerParams(
                collective_id=0, has_side_effects=True, vmem_limit_bytes=60 * 1024 * 1024
            ),
        )(sketch, far_tiles, jnp.transpose(row_blocks, (0, 2, 1, 3)), owner_route, cluster_basis)
        return coefficients[None, None]

    placed = (
        P("blk", None),
        P("blk", "group", None, None, None, None),
        P("blk", "group", None, None),
        P("blk", "group", None),
        P("blk", "group", None, None),
    )
    return jax.shard_map(
        body, mesh=mesh, in_specs=placed, out_specs=P("blk", "group", None, None), check_vma=False
    )
```

```python
import functools

import jax
import jax.numpy as jnp
from jax import lax
from jax.experimental import pallas as pl
from jax.experimental.pallas import tpu as pltpu
from jax.sharding import PartitionSpec as P

MESH = pl.DeviceIdType.MESH
LANES = 4
ROW = 2 * LANES
WIDTH = 128
BAND = 256
PARTS = (1, 2, 3)


def kernel(
    blks, groups,
    sketch, far_tiles, row_blocks, owner_route, cluster_basis, out,
    window, tiles, lefts, ordered, received, basis, basis_t,
    in_sem, halo_send, halo_recv, piece_send, piece_recv, across_send, across_recv,
    block_send, block_recv, present,
):
    b = lax.axis_index("blk")
    g = lax.axis_index("group")
    offsets, slots, tile_rows, panels = far_tiles.shape[2:]
    chunks = window.shape[0]
    half = groups // 2
    core = lax.rem(b, 2)
    low, high = lax.rem(b, ROW) == 0, lax.rem(b, ROW) == ROW - 1
    edge = low | high
    end = (g == 0) | (g == groups - 1)
    before, after = lax.rem(b + blks - 1, blks), lax.rem(b + 1, blks)
    piece = panels // LANES
    row = b // ROW * ROW
    lane = lax.rem(b, ROW) // 2
    held = jnp.where(edge, 1, offsets)
    splits, forwards = edge & end, end & jnp.logical_not(edge)
    goal = jnp.where(core == 0, lax.rem(row + blks - 1, blks), lax.rem(row + ROW, blks))
    feeders = jnp.where(low, lax.rem(row + blks - ROW, blks), lax.rem(row + ROW, blks)) + 1 - core

    flip = lax.rem(row // ROW, 2) == 1
    rank = jnp.where(flip, jnp.where(g < half, g + half, groups - 1 - g), g)

    def at_rank(r):
        return jnp.where(flip, jnp.where(r < half, groups - 1 - r, r - half), r)

    together = lane == LANES - 1

    starts = [sum(PARTS[:p]) for p in range(len(PARTS))]

    def own_chunk(k):
        return pltpu.make_async_copy(
            sketch.at[:, pl.ds(k * WIDTH, WIDTH)], window.at[k, 1], in_sem.at[k]
        )

    tiles_in = pltpu.make_async_copy(
        far_tiles.at[0, 0], tiles.at[:, pl.ds(0, slots)], in_sem.at[chunks]
    )
    basis_in = pltpu.make_async_copy(cluster_basis.at[0, 0], basis, in_sem.at[chunks + 1])

    def to_before(k):
        return pltpu.make_async_remote_copy(
            src_ref=window.at[k, 1], dst_ref=window.at[k, 2],
            send_sem=halo_send.at[0, k], recv_sem=halo_recv.at[1, k],
            device_id=(before, g), device_id_type=MESH,
        )

    def to_after(k):
        return pltpu.make_async_remote_copy(
            src_ref=window.at[k, 1], dst_ref=window.at[k, 0],
            send_sem=halo_send.at[1, k], recv_sem=halo_recv.at[0, k],
            device_id=(after, g), device_id_type=MESH,
        )

    def spread(p, step):
        lane_to = lax.rem(lane + step, LANES)
        rows = pl.ds(pl.multiple_of(lane_to * piece, piece), piece)
        span = pl.ds(starts[p], PARTS[p])
        return pltpu.make_async_remote_copy(
            src_ref=window.at[span, 1, rows], dst_ref=window.at[span, offsets, rows],
            send_sem=piece_send.at[p, step], recv_sem=piece_recv.at[p],
            device_id=(row + 2 * lane_to + core, g), device_id_type=MESH,
        )

    def across(p, hop):
        rows = pl.ds(pl.multiple_of(lane * piece, piece), piece)
        span = pl.ds(starts[p], PARTS[p])
        return pltpu.make_async_remote_copy(
            src_ref=window.at[span, held, rows], dst_ref=window.at[span, 2 * (1 - core), rows],
            send_sem=across_send.at[p, hop], recv_sem=across_recv.at[p],
            device_id=(goal, jnp.where(g == 0, groups - 1 - hop, hop)), device_id_type=MESH,
        )

    def from_across(p):
        span = pl.ds(starts[p], PARTS[p])
        return pltpu.make_async_remote_copy(
            src_ref=window.at[span, 1], dst_ref=window.at[span, 2 * core],
            send_sem=across_send.at[p, 0], recv_sem=across_recv.at[p],
            device_id=(goal, g), device_id_type=MESH,
        )

    def block(p, owner):
        span = pl.ds(starts[p], PARTS[p])
        return pltpu.make_async_remote_copy(
            src_ref=ordered.at[span, owner], dst_ref=received.at[span, g],
            send_sem=block_send.at[p, owner], recv_sem=block_recv.at[p, g],
            device_id=(b, owner), device_id_type=MESH,
        )

    def from_peer(p, peer):
        span = pl.ds(starts[p], PARTS[p])
        return pltpu.make_async_remote_copy(
            src_ref=ordered.at[span, peer], dst_ref=received.at[span, peer],
            send_sem=block_send.at[p, peer], recv_sem=block_recv.at[p, peer],
            device_id=(b, peer), device_id_type=MESH,
        )

    for k in range(chunks):
        own_chunk(k).start()
    tiles_in.start()
    barrier = pltpu.get_barrier_semaphore()

    def greet(blk, group):
        pl.semaphore_signal(barrier, inc=1, device_id=(blk, group), device_id_type=MESH)

    @pl.when(jnp.logical_not(low))
    def _():
        greet(before, g)

    @pl.when(jnp.logical_not(high))
    def _():
        greet(after, g)

    @pl.when(edge)
    def _():
        for q in range(LANES):
            greet(feeders + 2 * q, jnp.where(g < half, groups - 1, 0))

    @pl.when(forwards)
    def _():
        greet(row + core * (ROW - 1), g)

    for r in range(groups):

        @pl.when((r > rank) | (together & (r < rank)))
        def _():
            greet(b, at_rank(r))

    basis_in.start()
    tiles[:, slots] = jnp.zeros((offsets, tile_rows, panels), tiles.dtype)

    pl.semaphore_wait(
        barrier, jnp.where(together, groups - 1, rank) + jnp.where(edge, 1, 2) + jnp.where(end, half, 0) + jnp.where(splits, LANES - 1, 0)
    )

    for r in range(groups - 1):

        @pl.when((r < rank) & jnp.logical_not(together))
        def _():
            pl.semaphore_signal(
                present.at[g], inc=1, device_id=(b, at_rank(r)), device_id_type=MESH
            )

    for p, count in enumerate(PARTS):
        for k in range(starts[p], starts[p] + count):
            own_chunk(k).wait()

        @pl.when(splits)
        def _():
            for step in range(1, LANES):
                spread(p, step).start()
            for hop in range(half):
                across(p, hop).start()

        for k in range(starts[p], starts[p] + count):

            @pl.when(jnp.logical_not(low))
            def _():
                to_before(k).start()

            @pl.when(jnp.logical_not(high))
            def _():
                to_after(k).start()

    tiles_in.wait()
    for offset in range(offsets):
        owners = [owner_route[0, 0, row_blocks[0, offset, 0, slot]] for slot in range(slots)]
        for owner in range(groups):
            slot = jnp.int32(slots)
            for candidate in range(slots):
                slot = jnp.where(owners[candidate] == owner, candidate, slot)
            lefts[
                pl.ds(owner * tile_rows, tile_rows), pl.ds(offset * panels, panels)
            ] = tiles[offset, slot]

    per_band = BAND // tile_rows
    bands = groups // per_band

    def sample(k, sent):
        @pl.when(jnp.logical_not(low))
        def _():
            to_after(k).wait_recv()

        @pl.when(jnp.logical_not(high))
        def _():
            to_before(k).wait_recv()

        panels_in = window[k, 0:offsets].reshape(offsets * panels, WIDTH)

        if sent is not None:

            def one(r, _):
                owner = jnp.where(
                    together, lax.rem(r + jnp.where(g < half, half, 0), groups), at_rank(r)
                )
                ordered[k, owner] = jnp.dot(
                    lefts[pl.ds(pl.multiple_of(owner * tile_rows, tile_rows), tile_rows), :],
                    panels_in,
                    preferred_element_type=jnp.float32,
                ).astype(jnp.bfloat16)

                @pl.when((r > rank) & jnp.logical_not(together))
                def _():
                    pl.semaphore_wait(present.at[owner], 1)

                @pl.when(owner != g)
                def _():
                    block(sent, owner).start()

                return 0

            lax.fori_loop(0, groups, one, 0)
            received[k, g] = ordered[k, g]
            return 0

        def band(step, _):
            at = lax.rem(step + jnp.where(g < half, bands // 2, 0), bands)
            rows = jnp.dot(
                lefts[pl.ds(pl.multiple_of(at * BAND, BAND), BAND), :],
                panels_in,
                preferred_element_type=jnp.float32,
            ).astype(jnp.bfloat16)
            for part in range(per_band):
                owner = at * per_band + part
                ordered[k, owner] = rows[part * tile_rows : (part + 1) * tile_rows]
            return 0

        lax.fori_loop(0, bands, band, 0)
        received[k, g] = ordered[k, g]

        return 0

    for p, count in enumerate(PARTS):

        @pl.when(forwards)
        def _():
            spread(p, 0).wait_recv()
            for hop in range(half):
                across(p, hop).start()

        @pl.when(edge)
        def _():
            from_across(p).wait_recv()

        if count == 1:
            sample(starts[p], p)
            continue
        lax.fori_loop(starts[p], starts[p] + count, lambda k, _: sample(k, None), 0)

        def send(step, _):
            block(p, lax.rem(g + step, groups)).start()
            return 0

        lax.fori_loop(1, groups, send, 0)

    basis_in.wait()
    basis_t[...] = basis[...].T
    out[...] = jnp.zeros_like(out)

    for p in range(len(PARTS)):

        @pl.when(splits)
        def _():
            for step in range(1, LANES):
                spread(p, step).wait_send()

        @pl.when(end)
        def _():
            for hop in range(half):
                across(p, hop).wait_send()

    def drain(k, _):
        @pl.when(jnp.logical_not(low))
        def _():
            to_before(k).wait_send()

        @pl.when(jnp.logical_not(high))
        def _():
            to_after(k).wait_send()

        return 0

    lax.fori_loop(0, chunks, drain, 0)

    for p, count in enumerate(PARTS):

        def gather(step, _):
            near = step < half
            peer = jnp.where(g < half, 0, half) + lax.rem(g + step, half)
            peer = jnp.where(near, peer, lax.rem(peer + half, groups))

            @pl.when(step > 0)
            def _():
                from_peer(p, peer).wait_recv()

            part = basis_t[:, pl.ds(pl.multiple_of(peer * tile_rows, tile_rows), tile_rows)]
            for k in range(starts[p], starts[p] + count):
                out[:, k * WIDTH : (k + 1) * WIDTH] += jnp.dot(
                    part, received[k, peer], preferred_element_type=jnp.float32
                )
            return 0

        lax.fori_loop(0, groups, gather, 0)

    def drain_block(step, _):
        for p in range(len(PARTS)):
            block(p, lax.rem(g + step, groups)).wait_send()
        return 0

    lax.fori_loop(1, groups, drain_block, 0)


def solution(mesh):
    blks, groups = mesh.shape["blk"], mesh.shape["group"]

    def body(sketch, far_tiles, row_blocks, owner_route, cluster_basis):
        offsets, slots, tile_rows, panels = far_tiles.shape[2:]
        columns = sketch.shape[1]
        cluster_rows, rank = cluster_basis.shape[2:]
        chunks = columns // WIDTH
        kept = jnp.bfloat16
        coefficients = pl.pallas_call(
            functools.partial(kernel, blks, groups),
            out_shape=pltpu.VMEM((rank, columns), jnp.float32),
            in_specs=[
                pl.BlockSpec(memory_space=pl.ANY),
                pl.BlockSpec(memory_space=pl.ANY),
                pl.BlockSpec(memory_space=pltpu.SMEM),
                pl.BlockSpec(memory_space=pltpu.SMEM),
                pl.BlockSpec(memory_space=pl.ANY),
            ],
            out_specs=pl.BlockSpec(memory_space=pltpu.VMEM),
            scratch_shapes=[
                pltpu.VMEM((chunks, offsets + 1, panels, WIDTH), kept),
                pltpu.VMEM((offsets, slots + 1, tile_rows, panels), kept),
                pltpu.VMEM((groups * tile_rows, offsets * panels), kept),
                pltpu.VMEM((chunks, groups, tile_rows, WIDTH), kept),
                pltpu.VMEM((chunks, groups, tile_rows, WIDTH), kept),
                pltpu.VMEM((cluster_rows, rank), kept),
                pltpu.VMEM((rank, cluster_rows), kept),
                pltpu.SemaphoreType.DMA((chunks + 2,)),
                pltpu.SemaphoreType.DMA((2, chunks)),
                pltpu.SemaphoreType.DMA((2, chunks)),
                pltpu.SemaphoreType.DMA((len(PARTS), LANES)),
                pltpu.SemaphoreType.DMA((len(PARTS),)),
                pltpu.SemaphoreType.DMA((len(PARTS), groups // 2)),
                pltpu.SemaphoreType.DMA((len(PARTS),)),
                pltpu.SemaphoreType.DMA((len(PARTS), groups)),
                pltpu.SemaphoreType.DMA((len(PARTS), groups)),
                pltpu.SemaphoreType.REGULAR((groups,)),
            ],
            compiler_params=pltpu.CompilerParams(
                collective_id=0, has_side_effects=True, vmem_limit_bytes=60 * 1024 * 1024
            ),
        )(sketch, far_tiles, jnp.transpose(row_blocks, (0, 2, 1, 3)), owner_route, cluster_basis)
        return coefficients[None, None]

    placed = (
        P("blk", None),
        P("blk", "group", None, None, None, None),
        P("blk", "group", None, None),
        P("blk", "group", None),
        P("blk", "group", None, None),
    )
    return jax.shard_map(
        body, mesh=mesh, in_specs=placed, out_specs=P("blk", "group", None, None), check_vma=False
    )
```
